256 devices in a mesh: req: 16 (over y_hi, z), head: 16 (over y_lo, x, core).
Axes of the slice: x: 4, y: 4 (y_hi: 2, y_lo: 2; y = y_hi * 2 + y_lo), z: 8, core: 2. Of those that a mesh axis runs over, the one named last changes fastest.
Arguments:
- queries: bfloat16 [4096, 8192], P('req', 'head'), may hold values from -8 to 8
- new_keys: bfloat16 [4096, 1024], P('req'), may hold values from -5 to 5
- new_values: bfloat16 [4096, 1024], P('req'), may hold values from -24 to 24
- cache_keys: bfloat16 [32, 256, 1024], P('req'), may hold values from -4 to 4
- cache_values: bfloat16 [32, 256, 1024], P('req'), may hold values from -24 to 24
- request_slot: int32 [16], P('req'), may hold values from 0 to 1
- tenant_ids: int32 [4096], P('req'), may hold values from 0 to 255
- out_weight: bfloat16 [8192, 8192], P('req', 'head'), may hold values from -0.0625 to 0.0625
- adapter_down: bfloat16 [8192, 8192], P('head', 'req'), may hold values from -0.0625 to 0.0625
- adapter_up: bfloat16 [8192, 8192], P('req', 'head'), may hold values from -1 to 1
Outputs:
- mixed: bfloat16 [4096, 8192], P('req', 'head')
The draws below stay inside these ranges and needn't reach their ends.
All inputs are finite; a program needn't handle non-finite values.
Results may differ from the reference program's by a relative error of at most 0.0064.
Values may be sent and summed in bfloat16 or wider, within the bound.
No kernel may reach another device: no remote copies, remote signals or barrier semaphores. Data moves between devices by JAX's collectives and lax.ppermute only.
A program may use at most 128 MiB of HBM per device.

```python
import math
import jax
import jax.numpy as jnp
import numpy as np
from jax import lax

D = 8192
HEADS = 64
HD = 128
KVH = 8
RANK = 32
ROWS = 256
REQ_DEV = 2
KEYS = 256
TENANTS = 256
TOKENS = 4096
REQS = 32
N_REQ = 16


def draw_cache_keys(key, part):
    values = jnp.clip(jax.random.normal(jax.random.fold_in(key, 1), (REQS, KEYS, KVH * HD), jnp.float32), -4.0, 4.0)
    return values.astype(jnp.bfloat16)


def draw_queries(key, part):
    values = 1.5 * jnp.clip(jax.random.normal(jax.random.fold_in(key, 3), (TOKENS, HEADS * HD), jnp.float32), -4.0, 4.0)
    return values.astype(jnp.bfloat16)


def place_ends(result, rng, low, largest):
    spot = [jax.random.randint(jax.random.fold_in(rng, axis), (), 0, length) for axis, length in enumerate(result.shape)]
    longest = result.shape.index(max(result.shape))
    next_to = spot[:longest] + [(spot[longest] + 1) % result.shape[longest]] + spot[longest + 1:]
    return result.at[tuple(spot)].set(low).at[tuple(next_to)].set(largest)


def shard_levels(stream_key, shape, pieces, least, largest):
    factor_of, own = 1.0, jax.random.fold_in(stream_key, 6)
    for dim, blocks in pieces:
        draws = jnp.exp(jax.random.uniform(jax.random.fold_in(own, dim), (blocks,), jnp.float32, least / len(pieces), largest / len(pieces)))
        factor_of = factor_of * jnp.repeat(draws, shape[dim] // blocks).reshape([-1 if axis == dim else 1 for axis in range(len(shape))])
    return factor_of


def rank_bounds(number_of, skew):
    portions = [(1 << 20) // math.isqrt(standing ** skew) + 1 for standing in range(1, number_of + 1)]
    width = 1 + sum(portions) // (1 << 30)
    return np.cumsum(np.array([max(1, weight // width) for weight in portions]))


def skewed_ids(stream_key, dims, count, skew):
    listing = rank_bounds(count, skew)
    lot = jax.random.randint(jax.random.fold_in(stream_key, 1), dims, 0, int(listing[count - 1]))
    grade = jnp.searchsorted(jnp.asarray(listing, jnp.int32), lot, side="right")
    return jax.random.permutation(jax.random.fold_in(stream_key, 2), count)[grade].astype(jnp.int32)


def centred(rng, shape, spread, reach, cuts=(), kind=jnp.bfloat16):
    entries = spread * jax.random.normal(rng, shape, jnp.float32)
    if cuts:
        entries = entries * shard_levels(rng, shape, cuts, -0.22, 0.18)
    return jnp.clip(entries, -reach, reach).astype(kind)


def setup_inputs(seed: int = 0) -> dict:
    arg_keys = jax.random.split(jax.random.key(seed), 11)
    return {
        "queries": draw_queries(jax.random.fold_in(arg_keys[10], 71), 0),
        "new_keys": centred(arg_keys[1], (TOKENS, KVH * HD), 1.0, 5.0, ((0, 16),)),
        "new_values": centred(arg_keys[2], (TOKENS, KVH * HD), 4.0, 24.0, ((0, 16),)),
        "cache_keys": draw_cache_keys(jax.random.fold_in(arg_keys[10], 71), 0),
        "cache_values": centred(arg_keys[4], (REQS, KEYS, KVH * HD), 4.0, 24.0, ((0, 16),)),
        "request_slot": place_ends(jax.random.randint(arg_keys[5], (N_REQ,), 0, REQ_DEV), jax.random.fold_in(arg_keys[5], 1), 0, REQ_DEV - 1).astype(jnp.int32),
        "tenant_ids": place_ends(skewed_ids(arg_keys[6], (TOKENS,), TENANTS, 2), jax.random.fold_in(arg_keys[6], 3), 0, TENANTS - 1).astype(jnp.int32),
        "out_weight": centred(arg_keys[7], (D, D), D ** -0.5, 0.0625, ((0, 16), (1, 16))),
        "adapter_down": centred(arg_keys[8], (D, TENANTS * RANK), D ** -0.5, 0.0625, ((0, 16), (1, 16))),
        "adapter_up": centred(arg_keys[9], (TENANTS * RANK, D), RANK ** -0.5, 1.0, ((0, 16), (1, 16))),
    }


def settle(values):
    return lax.optimization_barrier(values.astype(jnp.bfloat16)).astype(jnp.float32)


def widen(block, count):
    group = HEADS // KVH
    return jnp.repeat(block.astype(jnp.float32).reshape(count, KVH, HD), group, axis=1)


def attend(block_queries, keys_old, values_old, keys_new, values_new):
    scale = HD ** -0.5
    queries = block_queries.astype(jnp.float32).reshape(ROWS, HEADS, HD)
    wide_keys_old = widen(keys_old, KEYS)
    wide_values_old = widen(values_old, KEYS)
    wide_keys_new = widen(keys_new, ROWS)
    wide_values_new = widen(values_new, ROWS)
    scores_old = jnp.einsum("qhd,khd->hqk", queries, wide_keys_old) * scale
    scores_new = jnp.einsum("qhd,khd->hqk", queries, wide_keys_new) * scale
    causal = jnp.arange(ROWS, dtype=jnp.int32)[:, None] >= jnp.arange(ROWS, dtype=jnp.int32)[None, :]
    scores_new = jnp.where(causal[None], scores_new, -1.0e30)
    highest = jnp.maximum(jnp.max(scores_old, axis=2), jnp.max(scores_new, axis=2))[:, :, None]
    weights_old = jnp.exp(scores_old - highest)
    weights_new = jnp.where(causal[None], jnp.exp(scores_new - highest), 0.0)
    total = jnp.sum(weights_old, axis=2, keepdims=True) + jnp.sum(weights_new, axis=2, keepdims=True)
    probs_old = settle(weights_old / total)
    probs_new = settle(weights_new / total)
    output = jnp.einsum("hqk,khd->qhd", probs_old, wide_values_old)
    output = output + jnp.einsum("hqk,khd->qhd", probs_new, wide_values_new)
    return output.reshape(ROWS, D).astype(jnp.bfloat16)


def reference(queries, new_keys, new_values, cache_keys, cache_values, request_slot, tenant_ids, out_weight, adapter_down, adapter_up):
    blocks = jnp.arange(N_REQ, dtype=jnp.int32)
    requests = blocks * REQ_DEV + request_slot.astype(jnp.int32)
    down_bank = adapter_down.reshape(D, TENANTS, RANK)
    up_bank = adapter_up.reshape(TENANTS, RANK, D)

    def per_block(index):
        start = (index * ROWS).astype(jnp.int32)
        request = lax.dynamic_index_in_dim(requests, index, 0, keepdims=False)
        attended = attend(
            lax.dynamic_slice_in_dim(queries, start, ROWS, 0),
            lax.dynamic_index_in_dim(cache_keys, request, 0, keepdims=False),
            lax.dynamic_index_in_dim(cache_values, request, 0, keepdims=False),
            lax.dynamic_slice_in_dim(new_keys, start, ROWS, 0),
            lax.dynamic_slice_in_dim(new_values, start, ROWS, 0))
        tenants = lax.dynamic_slice_in_dim(tenant_ids, start, ROWS, 0)
        down = jnp.take(down_bank, tenants, axis=1).astype(jnp.float32)
        shrunk = settle(jnp.einsum("rd,drk->rk", attended.astype(jnp.float32), down))
        lifted = jnp.take(up_bank, tenants, axis=0).astype(jnp.float32)
        delta = jnp.einsum("rk,rkd->rd", shrunk, lifted).astype(jnp.bfloat16)
        return attended, delta

    attended, delta = lax.map(per_block, blocks)
    attended = attended.reshape(TOKENS, D)
    delta = delta.reshape(TOKENS, D)
    base = jnp.dot(attended, out_weight, preferred_element_type=jnp.float32)
    return (base + lax.optimization_barrier(delta).astype(jnp.float32)).astype(jnp.bfloat16)
```

```python
import jax
import jax.numpy as jnp
from jax import lax
from jax.experimental import pallas as pl
from jax.experimental.pallas import tpu as pltpu
from jax.sharding import Mesh
from jax.sharding import PartitionSpec as P

HD = 128
RANK = 32
ROWS = 256
BF = jnp.bfloat16
F32 = jnp.float32
AXES = ("yh", "z", "yl", "x", "c")
REQ = ("yh", "z")
HEAD = ("yl", "x", "c")


def dot_nt(a, b):
    return lax.dot_general(a, b, (((1,), (1,)), ((), ())), preferred_element_type=F32)


def dot(a, b):
    return jnp.dot(a, b, preferred_element_type=F32)


def attend_kernel(where_ref, q_ref, ko_ref, vo_ref, kn_ref, vn_ref, out_ref):
    scale = HD**-0.5
    keys_old, values_old = ko_ref[0], vo_ref[0]
    keys_new, values_new = kn_ref[...], vn_ref[...]
    rows = q_ref.shape[0]
    causal = lax.broadcasted_iota(jnp.int32, (rows, rows), 0) >= lax.broadcasted_iota(
        jnp.int32, (rows, rows), 1
    )
    for head in range(q_ref.shape[1] // HD):
        cols = slice(head * HD, (head + 1) * HD)
        query = q_ref[:, cols]
        scores_old = dot_nt(query, keys_old) * scale
        scores_new = jnp.where(causal, dot_nt(query, keys_new) * scale, -1e30)
        highest = jnp.maximum(
            jnp.max(scores_old, axis=1, keepdims=True), jnp.max(scores_new, axis=1, keepdims=True)
        )
        weights_old = jnp.exp(scores_old - highest)
        weights_new = jnp.where(causal, jnp.exp(scores_new - highest), 0.0)
        total = jnp.sum(weights_old, axis=1, keepdims=True) + jnp.sum(
            weights_new, axis=1, keepdims=True
        )
        inverse = 1.0 / total
        probs_old = (weights_old * inverse).astype(BF)
        probs_new = (weights_new * inverse).astype(BF)
        out_ref[:, cols] = (dot(probs_old, values_old) + dot(probs_new, values_new)).astype(BF)


def attend(queries, new_keys, new_values, cache_keys, cache_values, where):
    rows, width = queries.shape
    keys = cache_keys.shape[1]
    return pl.pallas_call(
        attend_kernel,
        out_shape=jax.ShapeDtypeStruct((rows, width), BF),
        grid_spec=pltpu.PrefetchScalarGridSpec(
            num_scalar_prefetch=1,
            grid=(1,),
            in_specs=[
                pl.BlockSpec((rows, width), lambda i, w: (0, 0)),
                pl.BlockSpec((1, keys, HD), lambda i, w: (w[0], 0, w[1])),
                pl.BlockSpec((1, keys, HD), lambda i, w: (w[0], 0, w[1])),
                pl.BlockSpec((rows, HD), lambda i, w: (0, w[1])),
                pl.BlockSpec((rows, HD), lambda i, w: (0, w[1])),
            ],
            out_specs=pl.BlockSpec((rows, width), lambda i, w: (0, 0)),
        ),
        name="attend",
    )(where, queries, cache_keys, cache_values, new_keys, new_values)


def fold(value):
    value = value + pltpu.roll(value, 64, 1)
    return value + pltpu.roll(value, 32, 1)


def lane_group(shape):
    return lax.broadcasted_iota(jnp.int32, shape, 1) // RANK


def shrink_kernel(base_ref, att_ref, down_a_ref, down_b_ref, ids_ref, out_ref):
    step = pl.program_id(0)
    ids = ids_ref[...].astype(F32).astype(jnp.int32)
    group = lane_group(ids.shape)
    total = jnp.zeros(ids.shape, F32)
    for which, down_ref in enumerate((down_a_ref, down_b_ref)):
        product = dot(att_ref[...], down_ref[...])
        local = ids - base_ref[which]
        for part in range(product.shape[1] // 128):
            hit = local == group + part * 4
            total = total + jnp.where(hit, product[:, part * 128 : (part + 1) * 128], 0.0)
    total = jnp.where(group == step // 2, fold(total), 0.0)
    half = pl.ds(pl.multiple_of((step % 2) * ROWS, ROWS), ROWS)

    @pl.when(step < 2)
    def _():
        out_ref[half, :] = total

    @pl.when(step >= 2)
    def _():
        out_ref[half, :] += total


def shrink(attended, down_a, down_b, ids, bases):
    depth, width = down_a.shape
    return pl.pallas_call(
        shrink_kernel,
        out_shape=jax.ShapeDtypeStruct((2 * ROWS, 128), F32),
        grid_spec=pltpu.PrefetchScalarGridSpec(
            num_scalar_prefetch=1,
            grid=(8,),
            in_specs=[
                pl.BlockSpec((ROWS, depth), lambda i, w: (i, 0)),
                pl.BlockSpec((depth, width), lambda i, w: (0, 0)),
                pl.BlockSpec((depth, width), lambda i, w: (0, 0)),
                pl.BlockSpec((ROWS, 128), lambda i, w: (i, 0)),
            ],
            out_specs=pl.BlockSpec((2 * ROWS, 128), lambda i, w: (0, 0)),
        ),
        name="shrink",
    )(bases, attended, down_a, down_b, ids)


def project_kernel(
    base_ref, att_a_ref, att_b_ref, w_a_ref, w_b_ref, up_a_ref, up_b_ref, small_ref, ids_ref, out_ref
):
    step = pl.program_id(0)
    ids = ids_ref[...].astype(F32).astype(jnp.int32)
    group = lane_group(ids.shape)
    half = pl.ds(pl.multiple_of((step % 2) * ROWS, ROWS), ROWS)
    small = small_ref[half, :].astype(F32)
    small = fold(jnp.where(group == step // 2, small, 0.0))
    delta = jnp.zeros(out_ref.shape, F32)
    for which, up_ref in enumerate((up_a_ref, up_b_ref)):
        local = ids - base_ref[which]
        spread = [
            jnp.where(local == group + part * 4, small, 0.0).astype(BF)
            for part in range(up_ref.shape[0] // 128)
        ]
        delta = delta + dot(jnp.concatenate(spread, axis=1), up_ref[...])
    base = dot(att_a_ref[0], w_a_ref[...]) + dot(att_b_ref[0], w_b_ref[...])
    out_ref[...] = base + delta.astype(BF).astype(F32)


def project(gathered, w_a, w_b, up_a, up_b, small, ids, bases):
    depth, width = w_a.shape
    whole = pl.BlockSpec((depth, width), lambda i, w: (0, 0))
    return pl.pallas_call(
        project_kernel,
        out_shape=jax.ShapeDtypeStruct((8 * ROWS, width), F32),
        grid_spec=pltpu.PrefetchScalarGridSpec(
            num_scalar_prefetch=1,
            grid=(8,),
            in_specs=[
                pl.BlockSpec((1, ROWS, depth), lambda i, w: (w[2] * 8 + i, 0, 0)),
                pl.BlockSpec((1, ROWS, depth), lambda i, w: ((1 - w[2]) * 8 + i, 0, 0)),
                whole,
                whole,
                whole,
                whole,
                pl.BlockSpec((2 * ROWS, 128), lambda i, w: (0, 0)),
                pl.BlockSpec((ROWS, 128), lambda i, w: (i, 0)),
            ],
            out_specs=pl.BlockSpec((ROWS, width), lambda i, w: (i, 0)),
        ),
        name="project",
    )(bases, gathered, gathered, w_a, w_b, up_a, up_b, small, ids)


SWAP = [(0, 1), (1, 0)]
TURN = [
    (z * 8 + x * 2 + c, (x * 2 + c) * 8 + z) for z in range(8) for x in range(4) for c in range(2)
]


def local(
    queries,
    new_keys,
    new_values,
    cache_keys,
    cache_values,
    request_slot,
    tenant_ids,
    out_weight,
    adapter_down,
    adapter_up,
):
    yh, z = lax.axis_index("yh"), lax.axis_index("z")
    head = lax.axis_index(HEAD)
    tenants = adapter_up.shape[0] // RANK
    bases = jnp.stack([(yh * 8 + z) * tenants, ((1 - yh) * 8 + z) * tenants, yh]).astype(jnp.int32)
    where = jnp.stack([request_slot[0], head // 2]).astype(jnp.int32)

    down_b = lax.ppermute(adapter_down, "yh", SWAP)
    w_b = lax.ppermute(out_weight, "yh", SWAP)
    up_b = lax.ppermute(adapter_up, "yh", SWAP)
    ids = jnp.broadcast_to(tenant_ids[:, None], (ROWS, 128)).astype(BF)
    ids = lax.all_gather(lax.optimization_barrier(ids), "z", axis=0, tiled=True)

    attended = attend(queries, new_keys, new_values, cache_keys, cache_values, where)
    in_place = lax.all_gather(attended, "z", axis=0, tiled=True)
    turned = lax.ppermute(attended, ("z", "x", "c"), TURN)
    gathered = lax.all_gather(turned, HEAD, axis=0, tiled=False)

    packed = shrink(in_place, adapter_down, down_b, ids, bases)
    pieces = lax.all_to_all(packed.reshape(16, 32, 128), HEAD, 0, 0, tiled=False)
    small = jnp.sum(pieces, axis=0).astype(BF)
    small = lax.all_gather(small, HEAD, axis=0, tiled=True)

    partial_sum = project(gathered, out_weight, w_b, adapter_up, up_b, small, ids, bases)
    mixed = lax.psum_scatter(partial_sum, "z", scatter_dimension=0, tiled=True)
    return mixed.astype(BF)


def solution(mesh):
    fine = Mesh(mesh.devices.reshape(2, 8, 2, 4, 2), AXES)
    placed = (
        P(REQ, HEAD),
        P(REQ, None),
        P(REQ, None),
        P(REQ, None, None),
        P(REQ, None, None),
        P(REQ),
        P(REQ),
        P(REQ, HEAD),
        P(HEAD, REQ),
        P(REQ, HEAD),
    )
    return jax.shard_map(
        local, mesh=fine, in_specs=placed, out_specs=P(REQ, HEAD), check_vma=False
    )
```

```python
import functools

import jax
import jax.numpy as jnp
from jax import lax
from jax.experimental import pallas as pl
from jax.experimental.pallas import tpu as pltpu
from jax.sharding import Mesh
from jax.sharding import PartitionSpec as P

HD = 128
RANK = 32
ROWS = 256
HALF = 128
EXT = 8
BF = jnp.bfloat16
F32 = jnp.float32
AXES = ("yh", "z", "yl", "x", "c")
REQ = ("yh", "z")
HEAD = ("yl", "x", "c")
NZ = 8
NX = 4
SWAP = [(0, 1), (1, 0)]
VMEM = pl.BlockSpec(memory_space=pltpu.VMEM)
SMEM = pl.BlockSpec(memory_space=pltpu.SMEM)


def dot_nt(a, b):
    return lax.dot_general(a, b, (((1,), (1,)), ((), ())), preferred_element_type=F32)


def dot(a, b):
    return jnp.dot(a, b, preferred_element_type=F32)


def attend_kernel(
    where_ref, q_ref, ko_ref, vo_ref, kn_ref, vn_ref, ids_ref, ext_ref, pieces_ref
):
    scale = HD**-0.5
    keys_old, values_old = ko_ref[0], vo_ref[0]
    keys_new, values_new = kn_ref[...], vn_ref[...]
    rows = q_ref.shape[0]
    ids = jnp.broadcast_to(ids_ref[...].astype(F32), (EXT, rows)).astype(BF)
    ext_ref[:EXT, :rows] = ids
    ext_ref[:EXT, rows:] = ids
    causal = lax.broadcasted_iota(jnp.int32, (rows, rows), 0) >= lax.broadcasted_iota(
        jnp.int32, (rows, rows), 1
    )
    for head in range(q_ref.shape[1] // HD):
        cols = slice(head * HD, (head + 1) * HD)
        query = q_ref[:, cols]
        scores_old = dot_nt(query, keys_old) * scale
        scores_new = jnp.where(causal, dot_nt(query, keys_new) * scale, -1e30)
        highest = jnp.maximum(
            jnp.max(scores_old, axis=1, keepdims=True), jnp.max(scores_new, axis=1, keepdims=True)
        )
        weights_old = jnp.exp(scores_old - highest)
        weights_new = jnp.where(causal, jnp.exp(scores_new - highest), 0.0)
        total = jnp.sum(weights_old, axis=1, keepdims=True) + jnp.sum(
            weights_new, axis=1, keepdims=True
        )
        inverse = 1.0 / total
        probs_old = (weights_old * inverse).astype(BF)
        probs_new = (weights_new * inverse).astype(BF)
        out = (dot(probs_old, values_old) + dot(probs_new, values_new)).astype(BF)
        ext_ref[EXT:, cols] = out
        parity = where_ref[2]
        pieces_ref[parity, :, cols] = out[:HALF]
        pieces_ref[1 - parity, :, cols] = out[HALF:]


def attend(queries, new_keys, new_values, cache_keys, cache_values, ids, where):
    rows, width = queries.shape
    keys = cache_keys.shape[1]
    return pl.pallas_call(
        attend_kernel,
        out_shape=(
            jax.ShapeDtypeStruct((EXT + rows, width), BF),
            jax.ShapeDtypeStruct((2, HALF, width), BF),
        ),
        grid_spec=pltpu.PrefetchScalarGridSpec(
            num_scalar_prefetch=1,
            grid=(1,),
            in_specs=[
                pl.BlockSpec((rows, width), lambda i, w: (0, 0)),
                pl.BlockSpec((1, keys, HD), lambda i, w: (w[0], 0, w[1])),
                pl.BlockSpec((1, keys, HD), lambda i, w: (w[0], 0, w[1])),
                pl.BlockSpec((rows, HD), lambda i, w: (0, w[1])),
                pl.BlockSpec((rows, HD), lambda i, w: (0, w[1])),
                pl.BlockSpec((1, rows), lambda i, w: (0, 0)),
            ],
            out_specs=[
                pl.BlockSpec((EXT + rows, width), lambda i, w: (0, 0)),
                pl.BlockSpec((2, HALF, width), lambda i, w: (0, 0, 0)),
            ],
        ),
        name="attend",
    )(where, queries, cache_keys, cache_values, new_keys, new_values, ids)


def fold(value):
    value = value + pltpu.roll(value, 64, 1)
    return value + pltpu.roll(value, 32, 1)


def lane_group(shape):
    return lax.broadcasted_iota(jnp.int32, shape, 1) // RANK


def column(row):
    square = (HALF, HALF)
    diagonal = lax.broadcasted_iota(jnp.int32, square, 0) == lax.broadcasted_iota(
        jnp.int32, square, 1
    )
    picked = jnp.where(diagonal, jnp.broadcast_to(row, square), 0.0)
    return jnp.broadcast_to(jnp.sum(picked, axis=1, keepdims=True), square)


def shrink_kernel(offsets, split, with_total, scalar_ref, *refs):
    refs = list(refs)
    down_refs = refs[:2]
    chunks = refs[2 : 2 + (2 if split else len(offsets))]
    rest = refs[2 + len(chunks) :]
    total_ref = rest.pop(0) if with_total else None
    out_ref, codes_ref = rest
    if with_total:
        out_ref[...] = total_ref[...]
    else:
        out_ref[...] = jnp.zeros(out_ref.shape, F32)
    group = lane_group((HALF, HALF))
    core = scalar_ref[2]
    for index, offset in enumerate(offsets):
        for side in range(2):
            if split:
                block = chunks[side][EXT:, :] if side == 0 else chunks[side][...]
                row = chunks[0][:1, side * HALF : (side + 1) * HALF]
            else:
                start = EXT + side * HALF
                block = chunks[index][start : start + HALF, :]
                row = chunks[index][:1, side * HALF : (side + 1) * HALF]
            ids = column(row.astype(F32))

            @pl.when(core == side)
            def _():
                codes_ref[index] = ids

            ids = ids.astype(jnp.int32)
            total = jnp.zeros((HALF, HALF), F32)
            for which in range(2):
                product = dot(block, down_refs[which][...])
                local = ids - scalar_ref[which]
                for part in range(product.shape[1] // HALF):
                    hit = local == group + part * 4
                    total = total + jnp.where(
                        hit, product[:, part * HALF : (part + 1) * HALF], 0.0
                    )
            out_ref[side, offset // 4] += jnp.where(group == offset % 4, fold(total), 0.0)


def shrink(offsets, chunks, down_a, down_b, scalars, total=None):
    split = len(chunks) != len(offsets)
    extra = () if total is None else (total,)
    return pl.pallas_call(
        functools.partial(shrink_kernel, offsets, split, total is not None),
        out_shape=(
            jax.ShapeDtypeStruct((2, 2, HALF, HALF), F32),
            jax.ShapeDtypeStruct((len(offsets), HALF, HALF), F32),
        ),
        in_specs=[SMEM] + [VMEM] * (2 + len(chunks) + len(extra)),
        out_specs=[VMEM, VMEM],
        name="shrink" + "_".join(str(o) for o in offsets),
    )(scalars, down_a, down_b, *chunks, *extra)


def base_kernel(order_ref, g_ref, w_a_ref, w_b_ref, w_ac_ref, w_bc_ref, out_ref):
    swap = order_ref[NZ]
    first, second = g_ref[swap, 0], g_ref[1 - swap, 0]
    width = w_a_ref.shape[1]
    out_ref[0, :, :width] = dot(first, w_a_ref[...]) + dot(second, w_b_ref[...])
    out_ref[0, :, width:] = dot(first, w_ac_ref[...]) + dot(second, w_bc_ref[...])


def base_product(gathered, weights, order):
    depth, width = weights[0].shape
    whole = pl.BlockSpec((depth, width), lambda i, w: (0, 0))
    return pl.pallas_call(
        base_kernel,
        out_shape=jax.ShapeDtypeStruct((NZ, HALF, 2 * width), F32),
        grid_spec=pltpu.PrefetchScalarGridSpec(
            num_scalar_prefetch=1,
            grid=(NZ,),
            in_specs=[pl.BlockSpec((2, 1, HALF, depth), lambda i, w: (0, w[i], 0, 0))]
            + [whole] * 4,
            out_specs=pl.BlockSpec((1, HALF, 2 * width), lambda i, w: (i, 0, 0)),
        ),
        name="base",
    )(order, gathered, *weights)


def step_kernel(offsets, kind, scalar_ref, *refs):
    refs = list(refs)
    base_refs = [refs.pop(0) for _ in offsets]
    small_ref = refs.pop(0)
    codes_refs = [refs.pop(0) for _ in offsets]
    up_refs = [refs.pop(0) for _ in range(4)]
    arrived = [] if kind == "first" else [refs.pop(0) for _ in range(2)]
    outs = refs
    group = lane_group((HALF, HALF))
    width = up_refs[0].shape[1]
    for index, offset in enumerate(offsets):
        small = small_ref[offset // 4].astype(F32)
        small = fold(jnp.where(group == offset % 4, small, 0.0))
        ids = codes_refs[index][0].astype(jnp.int32)
        spread = []
        for which in range(2):
            local = ids - scalar_ref[which]
            spread.append(
                jnp.concatenate(
                    [
                        jnp.where(local == group + part * 4, small, 0.0).astype(BF)
                        for part in range(up_refs[0].shape[0] // HALF)
                    ],
                    axis=1,
                )
            )
        for core in range(2):
            cols = slice(core * width, (core + 1) * width)
            delta = dot(spread[0], up_refs[2 * core][...]) + dot(
                spread[1], up_refs[2 * core + 1][...]
            )
            value = base_refs[index][0, :, cols] + delta.astype(BF).astype(F32)
            quarter = HALF // 2
            if kind == "first":
                outs[0][:, cols] = value[:quarter].astype(BF)
                outs[1][:, cols] = value[quarter:].astype(BF)
            elif kind == "second":
                more = arrived[index][:, cols].astype(F32)
                if index == 0:
                    outs[0][:quarter, cols] = (value[:quarter] + more).astype(BF)
                    outs[0][quarter:, cols] = value[quarter:].astype(BF)
                else:
                    outs[1][:quarter, cols] = value[:quarter].astype(BF)
                    outs[1][quarter:, cols] = (value[quarter:] + more).astype(BF)
            elif kind == "next":
                outs[index][:, cols] = (value + arrived[index][:, cols].astype(F32)).astype(BF)
            else:
                value = value + arrived[0][:, cols].astype(F32)
                outs[core][...] = (value + arrived[1][:, cols].astype(F32)).astype(BF)


def chain_step(offsets, kind, scalars, base, small, codes, ups, arrived):
    width = ups[0].shape[1]
    if kind == "first":
        shapes = [(HALF // 2, 2 * width)] * 2
    elif kind == "last":
        shapes = [(HALF, width)] * 2
    else:
        shapes = [(HALF, 2 * width)] * 2
    tile = [
        pl.BlockSpec((1, HALF, 2 * width), functools.partial(lambda o, i, w: (o, 0, 0), o))
        for o in offsets
    ]
    code = [
        pl.BlockSpec(
            (1, HALF, HALF), functools.partial(lambda k, i, w: (k, 0, 0), codes[o][1])
        )
        for o in offsets
    ]

    def whole(shape):
        return pl.BlockSpec(shape, lambda i, w: (0,) * len(shape))

    return pl.pallas_call(
        functools.partial(step_kernel, offsets, kind),
        out_shape=[jax.ShapeDtypeStruct(s, BF) for s in shapes],
        grid_spec=pltpu.PrefetchScalarGridSpec(
            num_scalar_prefetch=1,
            grid=(1,),
            in_specs=tile
            + [whole(small.shape)]
            + code
            + [VMEM] * 4
            + [VMEM] * len(arrived),
            out_specs=[VMEM, VMEM],
        ),
        name="step" + "_".join(str(o) for o in offsets),
    )(
        scalars,
        *[base] * len(offsets),
        small,
        *[codes[o][0] for o in offsets],
        *ups,
        *arrived,
    )


def ring(count, by):
    return [(i, (i + by) % count) for i in range(count)]


def along_z(value, by):
    return lax.ppermute(value, "z", ring(NZ, by))


def along_x(value, by):
    return lax.ppermute(value, "x", ring(NX, by))


def turn(value, flip):
    pairs = [
        (z * 8 + x * 2 + c, (x * 2 + c) * 8 + (z // 2) * 2 + ((z % 2) ^ flip))
        for z in range(NZ)
        for x in range(NX)
        for c in range(2)
    ]
    return lax.ppermute(value, ("z", "x", "c"), pairs)


def pick(index, first, second):
    return jnp.where(index == 0, first, second)


def local(
    queries,
    new_keys,
    new_values,
    cache_keys,
    cache_values,
    request_slot,
    tenant_ids,
    out_weight,
    adapter_down,
    adapter_up,
):
    yh, z, yl, x, c = (lax.axis_index(name).astype(jnp.int32) for name in AXES)
    head = yl * 8 + x * 2 + c
    tenants = adapter_up.shape[0] // RANK
    scalars = jnp.stack([(yh * 8 + z) * tenants, ((1 - yh) * 8 + z) * tenants, c])
    where = jnp.stack([request_slot[0], head // 2, z % 2])

    down_b = lax.ppermute(adapter_down, "yh", SWAP)
    w_b = lax.ppermute(out_weight, "yh", SWAP)
    up_b = lax.ppermute(adapter_up, "yh", SWAP)
    w_ac = lax.ppermute(out_weight, "c", SWAP)
    up_ac = lax.ppermute(adapter_up, "c", SWAP)
    w_bc = lax.ppermute(w_b, "c", SWAP)
    up_bc = lax.ppermute(up_b, "c", SWAP)

    ext, pieces = attend(
        queries, new_keys, new_values, cache_keys, cache_values, tenant_ids[None, :], where
    )

    args = (adapter_down, down_b, scalars)
    right, left = along_z(ext, 1), along_z(ext, -1)
    turned = jnp.concatenate([turn(pieces[0], 0), turn(pieces[1], 1)])
    total, code = shrink((0,), (ext,), *args)
    codes = {0: (code, 0)}
    for offset in (1, 2, 3):
        if offset < 3:
            next_right, next_left = along_z(right, 1), along_z(left, -1)
        else:
            next_right = along_z(right[: EXT + HALF], 1)
            next_left = along_z(left[EXT + HALF :], -1)
        total, code = shrink((offset, NZ - offset), (left, right), *args, total)
        codes[offset], codes[NZ - offset] = (code, 0), (code, 1)
        right, left = next_right, next_left
    total, code = shrink((4,), (right, left), *args, total)
    codes[4] = (code, 0)

    from_left, from_right = along_x(turned, 1), along_x(turned, -1)
    other = lax.ppermute(turned, "yl", SWAP)
    other_left, other_right = along_x(other, 1), along_x(other, -1)
    far_left = along_x(jnp.concatenate([from_left[:HALF], other_left[:HALF]]), 1)
    far_right = along_x(jnp.concatenate([from_right[HALF:], other_right[HALF:]]), -1)
    gathered = jnp.concatenate(
        [
            turned,
            from_right,
            far_left[:HALF],
            far_right[:HALF],
            from_left,
            other,
            other_right,
            far_left[HALF:],
            far_right[HALF:],
            other_left,
        ]
    ).reshape(2, NZ, HALF, -1)
    targets = (z + jnp.arange(NZ, dtype=jnp.int32)) % NZ
    places = ((targets // 2 - x) % NX) * 2 + (targets % 2) ^ c
    order = jnp.concatenate([places, (yh ^ yl)[None]]).astype(jnp.int32)
    base = base_product(gathered, (out_weight, w_b, w_ac, w_bc), order)

    part = pick(c, total[0], total[1]) + lax.ppermute(pick(c, total[1], total[0]), "c", SWAP)
    part = pick(yl, part[0], part[1]) + lax.ppermute(pick(yl, part[1], part[0]), "yl", SWAP)
    part = part + along_x(part, 1) + along_x(part, 2) + along_x(part, 3)
    mine = part.astype(BF)
    theirs = lax.ppermute(mine, "yl", SWAP)
    small = jnp.stack([pick(yl, mine, theirs), pick(yl, theirs, mine)])

    ups = (adapter_up, up_b, up_ac, up_bc)
    to_right, to_left = chain_step((4,), "first", scalars, base, small, codes, ups, ())
    for offset, kind in ((3, "second"), (2, "next"), (1, "next")):
        arrived = (along_z(to_right, 1), along_z(to_left, -1))
        to_right, to_left = chain_step(
            (offset, NZ - offset), kind, scalars, base, small, codes, ups, arrived
        )
    arrived = (along_z(to_right, 1), along_z(to_left, -1))
    keep, give = chain_step((0,), "last", scalars, base, small, codes, ups, arrived)
    got = lax.ppermute(give, "c", SWAP)
    return jnp.concatenate([pick(c, keep, got), pick(c, got, keep)])


def solution(mesh):
    fine = Mesh(mesh.devices.reshape(2, NZ, 2, NX, 2), AXES)
    placed = (
        P(REQ, HEAD),
        P(REQ, None),
        P(REQ, None),
        P(REQ, None, None),
        P(REQ, None, None),
        P(REQ),
        P(REQ),
        P(REQ, HEAD),
        P(HEAD, REQ),
        P(REQ, HEAD),
    )
    return jax.shard_map(
        local, mesh=fine, in_specs=placed, out_specs=P(REQ, HEAD), check_vma=False
    )
```
